32 devices in a mesh: groups: 2 (over y), sky: 16 (over z, x, core).
Axes of the slice: x: 2, y: 2, z: 4, core: 2. Of those that a mesh axis runs over, the one named last changes fastest.
Arguments:
- model: float32 [64, 6, 256, 128], P(('groups', 'sky')), parts along dimension 0, may hold values from 0 to 2
- exposures: bfloat16 [4096, 16, 128], P(('groups', 'sky')), parts along dimension 0, may hold values from -6 to 6
- inv_var: float32 [4096], P(('groups', 'sky')), parts along dimension 0, may hold values from 0.5 to 2
- step_size: float32 [6], replicated, may hold values from 0.2 to 0.6
- psf_taps: float32 [64, 56], P(('groups', 'sky')), parts along dimension 0, may hold values from 0.05 to 1
- exp_batch: int32 [4096], P(('groups', 'sky')), parts along dimension 0, may hold values from 0 to 31
- send_plane: int32 [512, 16], P(('groups', 'sky')), parts along dimension 0, may hold values from -1 to 11, as said below
- send_row: int32 [512, 16], P(('groups', 'sky')), parts along dimension 0, may hold values from 0 to 248, as said below
- send_cover: int32 [512, 16], P(('groups', 'sky')), parts along dimension 0, may hold values from 0 to 16, as said below
- use_slot: int32 [4096, 2], P(('groups', 'sky')), parts along dimension 0, may hold values from -1 to 255, as said below
- use_start: int32 [4096, 2], P(('groups', 'sky')), parts along dimension 0, may hold values from 0 to 8, as said below
- use_stop: int32 [4096, 2], P(('groups', 'sky')), parts along dimension 0, may hold values from 0 to 16
- foot_lo: int32 [64], P(('groups', 'sky')), parts along dimension 0, may hold values from 0 to 63
- foot_hi: int32 [64], P(('groups', 'sky')), parts along dimension 0, may hold values from 193 to 256
Outputs:
- updated_model: float32 [64, 6, 256, 128], P(('groups', 'sky')), parts along dimension 0
- residual: float32 [4096, 16, 128], P(('groups', 'sky')), parts along dimension 0
The draws below stay inside these ranges and needn't reach their ends.
There are 2 independent parts, one for each index of `groups`. The reference program is written for one: setup_inputs(seed, part) draws one part's arguments, and reference() takes and returns one part's arrays. A program takes and returns all parts, laid end to end along the dimension named above; an argument that names none is the same for every part. Nothing has to cross between parts.
Inputs may be any that keep to these rules, and one draw needn't show every extreme that they name: In each row of send_plane the covered rows of the live slots (send_cover) sum to at most 128, and on every device some row reaches it. A live slot of exposure owner d is used by exactly one intersection of one exposure on d, and every intersection with use_slot >= 0 names a live slot; all pieces of an exposure come from planes of one band. `send_row`: for a live slot, the tile rows that its piece covers lie inside the tile. send_cover of a live slot equals use_stop - use_start of the intersection that uses it. `use_slot`: each exposure has 1 to 2 live intersections, first in order; -1 after them. `use_start`: the live intersections of an exposure cover rows 0 to 15 in order without gaps; dead ones have start and stop 0.
All inputs are finite; a program needn't handle non-finite values.
Results may differ from the reference program's by a relative error of at most 0.0011.
Values may be sent and summed in bfloat16 or wider, within the bound.
A program may use at most 128 MiB of HBM per device.

```python
import math
import jax
import jax.numpy as jnp
from jax import lax

B = 6
W = 128
TR = 256
H = 16
TILE_DEV = 2
EXP_DEV = 128
K = 2
NPSF = 4
TAPS = 7
ITERS = 2
NT = 32
NE = 2048
NBATCH = 32
CAP = 16
N_SKY = 16


def routing(key):
    base = jax.random.fold_in(key, 7919)
    keys = jax.random.split(base, 5)
    half = H // 2
    budget = CAP * H // 2
    count = jax.random.randint(keys[0], (N_SKY, EXP_DEV), 1, 3)
    count = count.at[:, 0].set(1)
    band_of = jax.random.randint(keys[1], (N_SKY, EXP_DEV), 0, B)
    source_order = jax.vmap(lambda subkey: jax.random.permutation(subkey, N_SKY))(jax.random.split(keys[2], N_SKY))
    tile_of = jax.random.randint(keys[3], (N_SKY, EXP_DEV, K), 0, TILE_DEV)
    raw_offset = jax.random.randint(keys[4], (N_SKY, EXP_DEV, K), 0, 1 << 20)
    intersection = jnp.arange(K, dtype=jnp.int32)[None, None, :]
    alive = intersection < count[:, :, None]
    split_two = count[:, :, None] == 2
    start = jnp.where(alive & (intersection == 1), half, 0)
    length = jnp.where(alive, jnp.where(split_two, jnp.where(intersection == 0, half, H - half), H), 0)
    stop = jnp.where(alive, start + length, 0)
    position = jnp.arange(EXP_DEV, dtype=jnp.int32)[None, :, None] * H + start
    source_rank = position // budget
    slot_column = position % budget // half
    source = jnp.take_along_axis(source_order, source_rank.reshape(N_SKY, -1), axis=1).reshape(N_SKY, EXP_DEV, K)
    slot = source * CAP + slot_column
    tile_row = raw_offset % (TR - length + 1)
    plane = tile_of * B + band_of[:, :, None]
    slot_alive = jnp.where(alive, slot, -1)
    target = jnp.where(alive, slot, N_SKY * CAP).reshape(N_SKY, -1)
    owners = jnp.arange(N_SKY, dtype=jnp.int32)[:, None]
    table_plane = jnp.full((N_SKY, N_SKY * CAP), -1, jnp.int32).at[owners, target].set(plane.reshape(N_SKY, -1), mode='drop')
    table_row = jnp.zeros((N_SKY, N_SKY * CAP), jnp.int32).at[owners, target].set(tile_row.reshape(N_SKY, -1), mode='drop')
    table_cover = jnp.zeros((N_SKY, N_SKY * CAP), jnp.int32).at[owners, target].set(length.reshape(N_SKY, -1), mode='drop')
    send_plane = table_plane.reshape(N_SKY, N_SKY, CAP).transpose(1, 0, 2).reshape(N_SKY * N_SKY, CAP)
    send_row = table_row.reshape(N_SKY, N_SKY, CAP).transpose(1, 0, 2).reshape(N_SKY * N_SKY, CAP)
    send_cover = table_cover.reshape(N_SKY, N_SKY, CAP).transpose(1, 0, 2).reshape(N_SKY * N_SKY, CAP)
    return (slot_alive.reshape(NE, K).astype(jnp.int32), start.reshape(NE, K).astype(jnp.int32), stop.reshape(NE, K).astype(jnp.int32), send_plane.astype(jnp.int32), send_row.astype(jnp.int32), send_cover.astype(jnp.int32))


def draw_use_slot(key, part):
    return routing(key)[0]


def draw_use_start(key, part):
    return routing(key)[1]


def draw_use_stop(key, part):
    return routing(key)[2]


def draw_send_plane(key, part):
    return routing(key)[3]


def draw_send_row(key, part):
    return routing(key)[4]


def draw_send_cover(key, part):
    return routing(key)[5]


def place_ends(drawn, stream_key, low, high):
    dims = drawn.shape
    place = [jax.random.randint(jax.random.fold_in(stream_key, axis), (), 0, dims[axis]) for axis in range(len(dims))]
    drawn = drawn.at[tuple(place)].set(low)
    longest = dims.index(max(dims))
    place[longest] = (place[longest] + 1) % dims[longest]
    return drawn.at[tuple(place)].set(high)


def levels(key, shape, cuts, low, top_value):
    def one(axis_at, shards_of):
        draws = jax.random.uniform(jax.random.fold_in(jax.random.fold_in(key, 6), axis_at), (shards_of,), jnp.float32, low / len(cuts), top_value / len(cuts))
        return jnp.repeat(jnp.exp(draws), shape[axis_at] // shards_of).reshape((-1,) + (1,) * (len(shape) - axis_at - 1))

    loudness = one(*cuts[0])
    for cut in cuts[1:]:
        loudness = loudness * one(*cut)
    return loudness


def noise(stream_key, shape, width, most, cuts=(), kind=jnp.bfloat16):
    array = jax.random.normal(stream_key, shape, jnp.float32) * width
    if len(cuts) > 0:
        array = levels(stream_key, shape, cuts, -0.22, 0.18) * array
    return jnp.clip(array, min=-most, max=most).astype(kind)


def setup_inputs(seed: int = 0, part: int = 0) -> dict:
    splits = jax.random.split(jax.random.key(seed), 15)
    part_keys = jax.random.split(jax.random.fold_in(splits[14], part), 15)
    return {
        "model": jnp.clip(2.0 * jax.random.uniform(part_keys[0], (NT, B, TR, W), jnp.float32) ** levels(part_keys[0], (NT, B, TR, W), ((0, 16),), -0.2, 0.2), 0.0, 2.0),
        "exposures": noise(part_keys[1], (NE, H, W), 1.0, 6.0, ((0, 16),)),
        "inv_var": jnp.clip(jnp.exp(math.log(2.0) - 1.3862944 * jax.random.uniform(part_keys[2], (NE,), jnp.float32) ** levels(part_keys[2], (NE,), ((0, 16),), -0.2, 0.2)), 0.5, 2.0),
        "step_size": jnp.clip(jnp.exp(jax.random.uniform(splits[3], (B,), jnp.float32, math.log(0.2), math.log(0.6))), 0.2, 0.6),
        "psf_taps": jnp.clip(0.05 + 0.95 * jax.random.uniform(part_keys[4], (NBATCH, 2 * NPSF * TAPS), jnp.float32) ** levels(part_keys[4], (NBATCH, 2 * NPSF * TAPS), ((0, 16),), -0.2, 0.2), 0.05, 1.0),
        "exp_batch": place_ends(jax.random.randint(part_keys[5], (NE,), 0, NBATCH), jax.random.fold_in(part_keys[5], 1), 0, NBATCH - 1).astype(jnp.int32),
        "send_plane": draw_send_plane(jax.random.fold_in(jax.random.fold_in(splits[14], part), 71), part),
        "send_row": draw_send_row(jax.random.fold_in(jax.random.fold_in(splits[14], part), 71), part),
        "send_cover": draw_send_cover(jax.random.fold_in(jax.random.fold_in(splits[14], part), 71), part),
        "use_slot": draw_use_slot(jax.random.fold_in(jax.random.fold_in(splits[14], part), 71), part),
        "use_start": draw_use_start(jax.random.fold_in(jax.random.fold_in(splits[14], part), 71), part),
        "use_stop": draw_use_stop(jax.random.fold_in(jax.random.fold_in(splits[14], part), 71), part),
        "foot_lo": place_ends(jax.random.randint(part_keys[12], (NT,), 0, TR // 4), jax.random.fold_in(part_keys[12], 1), 0, (TR // 4) - 1).astype(jnp.int32),
        "foot_hi": place_ends(jax.random.randint(part_keys[13], (NT,), TR - TR // 4 + 1, TR + 1), jax.random.fold_in(part_keys[13], 1), TR - TR // 4 + 1, TR).astype(jnp.int32),
    }


def build_ops(kernel_taps, extent):
    half_width = kernel_taps.shape[-1] // 2
    offset_grid = lax.broadcasted_iota(jnp.int32, (extent, extent), 0) - lax.broadcasted_iota(jnp.int32, (extent, extent), 1) + half_width
    onehot = (offset_grid[:, :, None] == jnp.arange(kernel_taps.shape[-1], dtype=jnp.int32)[None, None, :]).astype(jnp.float32)
    return jnp.einsum("ejt,abt->ejab", kernel_taps, onehot, precision=lax.Precision.HIGHEST).astype(jnp.bfloat16)


def block_step(padded, exposures, inv_var, taps_rows, use_slot, use_start, use_stop, send_plane, send_row, send_cover, owner):
    f32 = jnp.float32
    kernel_taps = taps_rows.reshape(taps_rows.shape[0], 2, NPSF, TAPS)
    kernel_taps = kernel_taps / jnp.sum(kernel_taps, axis=-1, keepdims=True)
    row_ops = build_ops(kernel_taps[:, 0], H)
    col_ops = build_ops(kernel_taps[:, 1], W)
    alive = use_slot >= 0
    slot_safe = jnp.maximum(use_slot, 0)
    source = slot_safe // CAP
    column = slot_safe % CAP
    table_row = source * N_SKY + owner
    plane = send_plane[table_row, column]
    cover = send_cover[table_row, column]
    row_first = send_row[table_row, column] + H - use_start
    global_plane = source * (TILE_DEV * B) + jnp.maximum(plane, 0)

    def take_piece(plane_id, row_start):
        return lax.dynamic_slice(padded, (plane_id, row_start, jnp.int32(0)), (1, H, W))[0]

    pieces = jax.vmap(jax.vmap(take_piece))(global_plane, row_first)
    row_pos = jnp.arange(H, dtype=jnp.int32)
    ahead = row_pos[None, None, :] >= use_start[:, :, None]
    forward = ahead & (row_pos[None, None, :] < use_start[:, :, None] + cover[:, :, None]) & alive[:, :, None]
    covered = ahead & (row_pos[None, None, :] < use_stop[:, :, None]) & alive[:, :, None]
    stamps = jnp.sum(jnp.where(forward[..., None], pieces.astype(f32), 0.0), axis=1).astype(jnp.bfloat16)
    blurred = jnp.einsum("erd,ejcd->erjc", stamps.astype(f32), col_ops.astype(f32)).astype(jnp.bfloat16)
    predicted = jnp.einsum("ejrs,esjc->erc", row_ops.astype(f32), blurred.astype(f32)) / NPSF
    residual = inv_var[:, None, None] * (predicted - exposures.astype(f32))
    back = jnp.einsum("ejsr,esc->erjc", row_ops.astype(f32), residual.astype(jnp.bfloat16).astype(f32)).astype(jnp.bfloat16)
    correlated = (jnp.einsum("erjc,ejcd->erd", back.astype(f32), col_ops.astype(f32)) / NPSF).astype(jnp.bfloat16)
    contrib = jnp.where(covered[..., None], correlated[:, None].astype(f32), 0.0)
    target = jnp.where(alive, global_plane, NT * B)
    return residual, target, row_first, contrib


def reference(model, exposures, inv_var, step_size, psf_taps, exp_batch, send_plane, send_row, send_cover, use_slot, use_start, use_stop, foot_lo, foot_hi):
    taps_all = psf_taps[exp_batch]
    current = model
    row_pos = jnp.arange(H, dtype=jnp.int32)
    tile_pos = jnp.arange(TR, dtype=jnp.int32)
    inside = (tile_pos[None, :] >= foot_lo[:, None]) & (tile_pos[None, :] < foot_hi[:, None])
    residual_all = None
    for sweep in range(ITERS):
        planes = current.astype(jnp.bfloat16).reshape(NT * B, TR, W)
        padded = jnp.pad(planes, ((0, 0), (H, H), (0, 0)))

        def one_block(gradient, owner):
            first = owner * EXP_DEV
            residual, target, row_first, contrib = block_step(
                padded,
                lax.dynamic_slice_in_dim(exposures, first, EXP_DEV, 0),
                lax.dynamic_slice_in_dim(inv_var, first, EXP_DEV, 0),
                lax.dynamic_slice_in_dim(taps_all, first, EXP_DEV, 0),
                lax.dynamic_slice_in_dim(use_slot, first, EXP_DEV, 0),
                lax.dynamic_slice_in_dim(use_start, first, EXP_DEV, 0),
                lax.dynamic_slice_in_dim(use_stop, first, EXP_DEV, 0),
                send_plane, send_row, send_cover, owner)
            gradient = gradient.at[target[:, :, None], row_first[:, :, None] + row_pos[None, None, :]].add(contrib, mode="drop")
            return gradient, residual

        gradient, residual_all = lax.scan(one_block, jnp.zeros((NT * B, TR + 2 * H, W), jnp.float32), jnp.arange(N_SKY, dtype=jnp.int32))
        gradient = gradient[:, H:H + TR].reshape(NT, B, TR, W)
        updated = jnp.maximum(current - step_size[None, :, None, None] * gradient, 0.0)
        current = jnp.where(inside[:, None, :, None], updated, 0.0)
    return current, residual_all.reshape(NE, H, W)
```

```python
import functools

import jax
import jax.numpy as jnp
from jax import lax
from jax.experimental import pallas as pl
from jax.experimental.pallas import tpu as pltpu
from jax.sharding import PartitionSpec as P

NPSF = 4
TAPS = 7
ITERS = 2
LEAD = 8
F32 = jnp.float32
BF16 = jnp.bfloat16


def vmem():
    return pl.BlockSpec(memory_space=pltpu.VMEM)


def smem():
    return pl.BlockSpec(memory_space=pltpu.SMEM)


def pack_rows(image, packed, plane, row, cover, rows_each, tile_rows, height):
    peers, capacity = plane.shape

    def one_peer(o, carry):
        offset = o * rows_each
        for c in range(capacity):
            source = jnp.maximum(plane[o, c], 0) * tile_rows + row[o, c]
            packed[pl.ds(offset, height), :] = image[pl.ds(source, height), :]
            offset = offset + cover[o, c]
        return carry

    lax.fori_loop(0, peers, one_peer, 0)


def emit_packed(packed, out, rows_each):
    def one_peer(o, carry):
        start = pl.multiple_of(o * rows_each, 16)
        out[o, pl.ds(0, rows_each), :] = packed[pl.ds(start, rows_each), :].astype(BF16)
        return carry

    lax.fori_loop(0, out.shape[0], one_peer, 0)


def first_kernel(rows_each, tile_rows, height, plane, row, cover, model, banks, out, image, packed):
    total = model.shape[0]
    image[pl.ds(0, total), :] = model[...]
    image[pl.ds(total, height), :] = jnp.zeros((height, model.shape[1]), F32)
    pack_rows(image, packed, plane, row, cover, rows_each, tile_rows, height)
    emit_packed(packed, out, rows_each)
    extra = banks.shape[0]

    def add_banks(o, carry):
        out[o, pl.ds(rows_each, extra), :] = banks[...]
        return carry

    lax.fori_loop(0, out.shape[0], add_banks, 0)


def tile_kernel(rows_each, tile_rows, height, band_count, last, plane, row, cover, lo, hi, step, current,
                returned, *rest):
    if last:
        updated, grad, arrived = rest
    else:
        updated, out, grad, arrived, image, packed = rest
    total, columns = current.shape
    peers, capacity = plane.shape

    def clear(i, carry):
        start = pl.multiple_of(i * 64, 64)
        grad[pl.ds(start, 64), :] = jnp.zeros((64, columns), F32)
        return carry

    lax.fori_loop(0, total // 64, clear, 0)
    grad[pl.ds(total, height), :] = jnp.zeros((height, columns), F32)

    def widen(o, carry):
        start = pl.multiple_of(o * rows_each, 16)
        arrived[pl.ds(start, rows_each), :] = returned[o].astype(F32)
        return carry

    lax.fori_loop(0, peers, widen, 0)
    arrived[pl.ds(peers * rows_each, height), :] = jnp.zeros((height, columns), F32)
    position = lax.broadcasted_iota(jnp.int32, (height, columns), 0)

    def one_peer(o, carry):
        offset = o * rows_each
        for c in range(capacity):
            target = jnp.maximum(plane[o, c], 0) * tile_rows + row[o, c]
            count = cover[o, c]
            part = jnp.where(position < count, arrived[pl.ds(offset, height), :], 0.0)
            grad[pl.ds(target, height), :] += part
            offset = offset + count
        return carry

    lax.fori_loop(0, peers, one_peer, 0)
    tile_position = lax.broadcasted_iota(jnp.int32, (tile_rows, columns), 0)

    def one_plane(p, carry):
        tile = p // band_count
        start = pl.multiple_of(p * tile_rows, 8)
        here = pl.ds(start, tile_rows)
        moved = jnp.maximum(current[here, :] - step[p % band_count] * grad[here, :], 0.0)
        moved = jnp.where((tile_position >= lo[tile]) & (tile_position < hi[tile]), moved, 0.0)
        updated[here, :] = moved
        if not last:
            image[here, :] = moved
        return carry

    lax.fori_loop(0, total // tile_rows, one_plane, 0)
    if not last:
        image[pl.ds(total, height), :] = jnp.zeros((height, columns), F32)
        pack_rows(image, packed, plane, row, cover, rows_each, tile_rows, height)
        emit_packed(packed, out, rows_each)


def convolve(image, base, taps, taps_base, direction, masks):
    height, columns = masks[0].shape
    half = TAPS // 2
    rows = [image[pl.ds(base - direction * (u - half), height), :] for u in range(TAPS)]
    total = None
    for v in range(TAPS):
        part = None
        for u in range(TAPS):
            term = taps[pl.ds(taps_base + (u * TAPS + v), 1), :] * rows[u]
            part = term if part is None else part + term
        shift = direction * (v - half)
        if shift != 0:
            part = jnp.where(masks[shift + half], pltpu.roll(part, shift % columns, 1), 0.0)
        total = part if total is None else total + part
    return total


def exposure_kernel(rows_each, bank_rows, unroll, slot, start, stop, batch, weight, arrived, taps, observed,
                    residual, out, gathered, stamps, errors, length, begin, source):
    count, height, columns = observed.shape
    peers = out.shape[0]
    meets = slot.shape[1]
    slots = length.shape[0]
    capacity = slots // peers
    pitch = height + LEAD
    half = TAPS // 2

    def clear_slots(i, carry):
        length[i] = 0
        source[i] = LEAD
        return carry

    lax.fori_loop(0, slots, clear_slots, 0, unroll=8)

    def mark(e, carry):
        for k in range(meets):
            name = slot[e, k]

            @pl.when(name >= 0)
            def _():
                first = start[e, k]
                length[name] = stop[e, k] - first
                source[name] = e * pitch + LEAD + first
        return carry

    lax.fori_loop(0, count, mark, 0, unroll=4)

    def prefix(o, carry):
        offset = o * rows_each
        for c in range(capacity):
            begin[o * capacity + c] = offset
            offset = offset + length[o * capacity + c]
        return carry

    lax.fori_loop(0, peers, prefix, 0)

    gathered[pl.ds(0, height), :] = jnp.zeros((height, columns), F32)
    gathered[pl.ds(height + peers * rows_each, height), :] = jnp.zeros((height, columns), F32)

    def widen(o, carry):
        here = pl.multiple_of(o * rows_each + height, 8)
        gathered[pl.ds(here, rows_each), :] = arrived[o, pl.ds(0, rows_each), :].astype(F32)
        return carry

    lax.fori_loop(0, peers, widen, 0)
    gap = jnp.zeros((LEAD, columns), F32)
    stamps[pl.ds(0, LEAD), :] = gap
    errors[pl.ds(0, LEAD), :] = gap
    position = lax.broadcasted_iota(jnp.int32, (height, columns), 0)

    def assemble(e, carry):
        value = None
        for k in range(meets):
            name = slot[e, k]
            alive = name >= 0
            first = jnp.where(alive, start[e, k], height)
            at = height + jnp.where(alive, begin[jnp.maximum(name, 0)] - first, 0)
            piece = gathered[pl.ds(at, height), :]
            value = piece if value is None else jnp.where(position >= first, piece, value)
        here = pl.multiple_of(e * pitch + LEAD, 8)
        stamps[pl.ds(here, height), :] = value
        stamps[pl.ds(here + height, LEAD), :] = gap
        errors[pl.ds(here + height, LEAD), :] = gap
        return carry

    lax.fori_loop(0, count, assemble, 0, unroll=8)
    lane = lax.broadcasted_iota(jnp.int32, (height, columns), 1)
    masks = [
        (lane >= shift) if shift > 0 else (lane < columns + shift) for shift in range(-half, half + 1)
    ]

    def group(g, carry):
        which = [g * unroll + i for i in range(unroll)]
        for e in which:
            here = pl.multiple_of(e * pitch + LEAD, 8)
            predicted = convolve(stamps, here, taps, batch[e] * bank_rows, 1, masks)
            error = weight[e] * (predicted - observed[e].astype(F32))
            residual[e] = error
            errors[pl.ds(here, height), :] = error.astype(BF16).astype(F32)
        for e in which:
            here = pl.multiple_of(e * pitch + LEAD, 8)
            stamps[pl.ds(here, height), :] = convolve(errors, here, taps, batch[e] * bank_rows, -1, masks)
        return carry

    lax.fori_loop(0, count // unroll, group, 0)

    def give(o, carry):
        for c in range(capacity):
            name = o * capacity + c
            gathered[pl.ds(begin[name], height), :] = stamps[pl.ds(source[name], height), :]
        return carry

    lax.fori_loop(0, peers, give, 0)
    emit_packed(gathered, out, rows_each)


def body(model, exposures, inv_var, step_size, psf_taps, exp_batch, send_plane, send_row, send_cover, use_slot,
         use_start, use_stop, foot_lo, foot_hi):
    tile_count, band_count, tile_rows, columns = model.shape
    count, height, _ = exposures.shape
    peers, capacity = send_plane.shape
    rows_each = capacity * height // 2
    total = tile_count * band_count * tile_rows
    packed_rows = peers * rows_each
    own_banks, width = psf_taps.shape
    extra = -(-own_banks // 16) * 16
    bank_rows = -(-TAPS * TAPS // 8) * 8
    unroll = 4 if count % 4 == 0 else 1

    shaped = psf_taps.reshape(own_banks, 2 * NPSF, TAPS)
    shaped = shaped / jnp.sum(shaped, axis=-1, keepdims=True)
    banks = shaped.reshape(own_banks, width).astype(BF16)
    banks = jnp.pad(banks, ((0, extra - own_banks), (0, columns - width)))

    image_scratch = pltpu.VMEM((total + height, columns), F32)
    packed_scratch = pltpu.VMEM((packed_rows + height, columns), F32)
    exchange = functools.partial(lax.all_to_all, axis_name="sky", split_axis=0, concat_axis=0, tiled=True)

    current = model.reshape(total, columns)
    outbound = pl.pallas_call(
        functools.partial(first_kernel, rows_each, tile_rows, height),
        out_shape=jax.ShapeDtypeStruct((peers, rows_each + extra, columns), BF16),
        in_specs=[smem()] * 3 + [vmem()] * 2,
        out_specs=vmem(),
        scratch_shapes=[image_scratch, packed_scratch],
        name="first_pack",
    )(send_plane, send_row, send_cover, current, banks)
    residual = None
    taps = None
    for sweep in range(ITERS):
        arrived = exchange(outbound)
        if sweep == 0:
            pool = arrived[:, rows_each : rows_each + own_banks, :width].astype(F32)
            pool = pool.reshape(peers * own_banks, 2, NPSF, TAPS)
            kernels = jnp.sum(pool[:, 0, :, :, None] * pool[:, 1, :, None, :], axis=1) / NPSF
            kernels = kernels.reshape(peers * own_banks, TAPS * TAPS)
            kernels = jnp.pad(kernels, ((0, 0), (0, bank_rows - TAPS * TAPS)))
            taps = jnp.broadcast_to(
                kernels.reshape(peers * own_banks * bank_rows, 1), (peers * own_banks * bank_rows, columns)
            )
        residual, outgoing = pl.pallas_call(
            functools.partial(exposure_kernel, rows_each, bank_rows, unroll),
            out_shape=(
                jax.ShapeDtypeStruct(exposures.shape, F32),
                jax.ShapeDtypeStruct((peers, rows_each, columns), BF16),
            ),
            in_specs=[smem()] * 5 + [vmem()] * 3,
            out_specs=(vmem(), vmem()),
            scratch_shapes=[
                pltpu.VMEM((packed_rows + 2 * height, columns), F32),
                pltpu.VMEM((LEAD + count * (height + LEAD), columns), F32),
                pltpu.VMEM((LEAD + count * (height + LEAD), columns), F32),
                pltpu.SMEM((peers * capacity,), jnp.int32),
                pltpu.SMEM((peers * capacity,), jnp.int32),
                pltpu.SMEM((peers * capacity,), jnp.int32),
            ],
            name="exposures",
        )(use_slot, use_start, use_stop, exp_batch, inv_var, arrived, taps, exposures)
        returned = exchange(outgoing)
        last = sweep == ITERS - 1
        updated_shape = jax.ShapeDtypeStruct((total, columns), F32)
        outbound_shape = jax.ShapeDtypeStruct((peers, rows_each, columns), BF16)
        result = pl.pallas_call(
            functools.partial(tile_kernel, rows_each, tile_rows, height, band_count, last),
            out_shape=updated_shape if last else (updated_shape, outbound_shape),
            in_specs=[smem()] * 6 + [vmem()] * 2,
            out_specs=vmem() if last else (vmem(), vmem()),
            scratch_shapes=[image_scratch, packed_scratch] + ([] if last else [image_scratch, packed_scratch]),
            name="tiles_last" if last else "tiles",
        )(send_plane, send_row, send_cover, foot_lo, foot_hi, step_size, current, returned)
        if last:
            current = result
        else:
            current, outbound = result
    return current.reshape(model.shape), residual


def solution(mesh):
    both = ("groups", "sky")
    return jax.shard_map(
        body,
        mesh=mesh,
        in_specs=(
            P(both, None, None, None),
            P(both, None, None),
            P(both),
            P(),
            P(both, None),
            P(both),
            P(both, None),
            P(both, None),
            P(both, None),
            P(both, None),
            P(both, None),
            P(both, None),
            P(both),
            P(both),
        ),
        out_specs=(P(both, None, None, None), P(both, None, None)),
        check_vma=False,
    )
```

```python
import functools

import jax
import jax.numpy as jnp
import numpy as np
from jax import lax
from jax.experimental import pallas as pl
from jax.experimental.pallas import tpu as pltpu
from jax.sharding import PartitionSpec as P

NPSF = 4
TAPS = 7
ITERS = 2
F32 = jnp.float32
BF16 = jnp.bfloat16


def vmem():
    return pl.BlockSpec(memory_space=pltpu.VMEM)


def smem():
    return pl.BlockSpec(memory_space=pltpu.SMEM)


def pack_rows(image, packed, plane, row, cover, rows_each, tile_rows, height):
    peers, capacity = plane.shape

    def one_peer(o, carry):
        offset = o * rows_each
        for c in range(capacity):
            source = jnp.maximum(plane[o, c], 0) * tile_rows + row[o, c]
            packed[pl.ds(offset, height), :] = image[pl.ds(source, height), :]
            offset = offset + cover[o, c]
        return carry

    lax.fori_loop(0, peers, one_peer, 0)


def emit_packed(packed, out, rows_each):
    def one_peer(o, carry):
        start = pl.multiple_of(o * rows_each, 16)
        out[o, pl.ds(0, rows_each), :] = packed[pl.ds(start, rows_each), :].astype(BF16)
        return carry

    lax.fori_loop(0, out.shape[0], one_peer, 0)


def first_kernel(rows_each, tile_rows, height, plane, row, cover, slot, start, stop, model, banks, out, begin, source,
                 image, packed, length):
    slot_tables(rows_each, height, out.shape[0], slot, start, stop, begin, source, length)
    total = model.shape[0]
    image[pl.ds(0, total), :] = model[...]
    image[pl.ds(total, height), :] = jnp.zeros((height, model.shape[1]), F32)
    pack_rows(image, packed, plane, row, cover, rows_each, tile_rows, height)
    emit_packed(packed, out, rows_each)
    extra = banks.shape[0]

    def add_banks(o, carry):
        out[o, pl.ds(rows_each, extra), :] = banks[...]
        return carry

    lax.fori_loop(0, out.shape[0], add_banks, 0)


def tile_kernel(rows_each, tile_rows, height, band_count, last, plane, row, cover, lo, hi, step, current,
                returned, *rest):
    if last:
        updated, grad, arrived = rest
    else:
        updated, out, grad, arrived, image, packed = rest
    total, columns = current.shape
    peers, capacity = plane.shape

    def clear(i, carry):
        start = pl.multiple_of(i * 64, 64)
        grad[pl.ds(start, 64), :] = jnp.zeros((64, columns), F32)
        return carry

    lax.fori_loop(0, total // 64, clear, 0)
    grad[pl.ds(total, height), :] = jnp.zeros((height, columns), F32)

    def widen(o, carry):
        start = pl.multiple_of(o * rows_each, 16)
        arrived[pl.ds(start, rows_each), :] = returned[o].astype(F32)
        return carry

    lax.fori_loop(0, peers, widen, 0)
    arrived[pl.ds(peers * rows_each, height), :] = jnp.zeros((height, columns), F32)
    position = lax.broadcasted_iota(jnp.int32, (height, columns), 0)

    def one_peer(o, carry):
        offset = o * rows_each
        for c in range(capacity):
            target = jnp.maximum(plane[o, c], 0) * tile_rows + row[o, c]
            count = cover[o, c]
            part = jnp.where(position < count, arrived[pl.ds(offset, height), :], 0.0)
            grad[pl.ds(target, height), :] += part
            offset = offset + count
        return carry

    lax.fori_loop(0, peers, one_peer, 0)
    tile_position = lax.broadcasted_iota(jnp.int32, (tile_rows, columns), 0)

    def one_plane(p, carry):
        tile = p // band_count
        start = pl.multiple_of(p * tile_rows, 8)
        here = pl.ds(start, tile_rows)
        moved = jnp.maximum(current[here, :] - step[p % band_count] * grad[here, :], 0.0)
        moved = jnp.where((tile_position >= lo[tile]) & (tile_position < hi[tile]), moved, 0.0)
        updated[here, :] = moved
        if not last:
            image[here, :] = moved
        return carry

    lax.fori_loop(0, total // tile_rows, one_plane, 0)
    if not last:
        image[pl.ds(total, height), :] = jnp.zeros((height, columns), F32)
        pack_rows(image, packed, plane, row, cover, rows_each, tile_rows, height)
        emit_packed(packed, out, rows_each)


def spread(value, target, direction, masks):
    height, columns = value.shape
    half = TAPS // 2
    for v in range(TAPS):
        shift = direction * (v - half)
        part = value
        if shift != 0:
            part = jnp.where(masks[shift + half], pltpu.roll(value, shift % columns, 1), 0.0)
        target[pl.ds(v * height, height), :] = part.astype(BF16)


def apply(operator, shifted):
    both = jnp.dot(operator, shifted, preferred_element_type=F32)
    height = both.shape[0] // 2
    return both[:height] + both[height:]


def exposure_kernel(rows_each, unroll, slot, start, batch, weight, begin, source, arrived, operators, observed,
                    residual, out, gathered, stamps, forward, backward):
    count, height, columns = observed.shape
    peers = out.shape[0]
    meets = slot.shape[1]
    capacity = begin.shape[0] // peers
    half = TAPS // 2

    gathered[pl.ds(0, height), :] = jnp.zeros((height, columns), F32)
    gathered[pl.ds(height + peers * rows_each, height), :] = jnp.zeros((height, columns), F32)
    stamps[pl.ds(count * height, height), :] = jnp.zeros((height, columns), F32)
    used = TAPS * height
    spare = forward.shape[1] - used
    if spare:
        for i in range(unroll):
            forward[i, pl.ds(used, spare), :] = jnp.zeros((spare, columns), BF16)
            backward[i, pl.ds(used, spare), :] = jnp.zeros((spare, columns), BF16)

    def widen(o, carry):
        here = pl.multiple_of(o * rows_each + height, 8)
        gathered[pl.ds(here, rows_each), :] = arrived[o, pl.ds(0, rows_each), :].astype(F32)
        return carry

    lax.fori_loop(0, peers, widen, 0)
    position = lax.broadcasted_iota(jnp.int32, (height, columns), 0)
    lane = lax.broadcasted_iota(jnp.int32, (height, columns), 1)
    masks = [
        (lane >= shift) if shift > 0 else (lane < columns + shift) for shift in range(-half, half + 1)
    ]

    def assemble(e):
        value = None
        for k in range(meets):
            name = slot[e, k]
            alive = name >= 0
            first = jnp.where(alive, start[e, k], height)
            at = height + jnp.where(alive, begin[jnp.maximum(name, 0)] - first, 0)
            piece = gathered[pl.ds(at, height), :]
            value = piece if value is None else jnp.where(position >= first, piece, value)
        return value

    def group(g, carry):
        which = [g * unroll + i for i in range(unroll)]
        for i, e in enumerate(which):
            spread(assemble(e), forward.at[i], 1, masks)
        for i, e in enumerate(which):
            predicted = apply(operators[batch[e], 0], forward[i])
            error = weight[e] * (predicted - observed[e].astype(F32))
            residual[e] = error
            spread(error, backward.at[i], -1, masks)
        for i, e in enumerate(which):
            here = pl.multiple_of(e * height, 8)
            stamps[pl.ds(here, height), :] = apply(operators[batch[e], 1], backward[i])
        return carry

    lax.fori_loop(0, count // unroll, group, 0)

    def give(o, carry):
        for c in range(capacity):
            name = o * capacity + c
            gathered[pl.ds(begin[name], height), :] = stamps[pl.ds(source[name], height), :]
        return carry

    lax.fori_loop(0, peers, give, 0)
    emit_packed(gathered, out, rows_each)


def slot_tables(rows_each, height, peers, slot, start, stop, begin, source, length):
    count, meets = slot.shape
    slots = begin.shape[0]
    capacity = slots // peers

    def clear_slots(i, carry):
        length[i] = 0
        source[i] = 0
        return carry

    lax.fori_loop(0, slots, clear_slots, 0, unroll=16)

    def mark(e, carry):
        for k in range(meets):
            name = slot[e, k]
            first = start[e, k]
            alive = name >= 0
            length[jnp.where(alive, name, slots)] = stop[e, k] - first
            name = jnp.where(alive, name, e * 0)
            source[name] = jnp.where(alive, e * height + first, source[name])
        return carry

    lax.fori_loop(0, count, mark, 0, unroll=8)

    def prefix(o, carry):
        offset = o * rows_each
        for c in range(capacity):
            begin[o * capacity + c] = offset
            offset = offset + length[o * capacity + c]
        return carry

    lax.fori_loop(0, peers, prefix, 0)


def partner(me, i, peers):
    if peers & (peers - 1):
        return lax.rem(me + i, peers)
    other = me
    bit = 1
    while bit < peers:
        if i & bit:
            other = other + (1 - 2 * lax.rem(me // bit, 2)) * bit
        bit *= 2
    return other


def exchange_kernel(outgoing, incoming, send_sems, recv_sems, own_sem):
    me = lax.axis_index("sky")
    peers = outgoing.shape[0]
    order = [base + d for base in range(0, peers, 4) for d in (2, 0, 3, 1) if 0 < base + d < peers]
    barrier = pltpu.get_barrier_semaphore()
    for i in order:
        pl.semaphore_signal(
            barrier, inc=1, device_id={"sky": partner(me, i, peers)}, device_id_type=pl.DeviceIdType.MESH
        )
    pl.semaphore_wait(barrier, peers - 1)
    copies = []
    for i in order:
        to = partner(me, i, peers)
        copy = pltpu.make_async_remote_copy(
            src_ref=outgoing.at[to],
            dst_ref=incoming.at[me],
            send_sem=send_sems.at[i],
            recv_sem=recv_sems.at[i],
            device_id={"sky": to},
            device_id_type=pl.DeviceIdType.MESH,
        )
        copy.start()
        copies.append(copy)
    own = pltpu.make_async_copy(outgoing.at[me], incoming.at[me], own_sem)
    own.start()
    own.wait()
    for copy in copies:
        copy.wait()


def exchange(outgoing, ident):
    peers = outgoing.shape[0]
    return pl.pallas_call(
        exchange_kernel,
        out_shape=jax.ShapeDtypeStruct(outgoing.shape, outgoing.dtype),
        in_specs=[pl.BlockSpec(memory_space=pl.ANY)],
        out_specs=pl.BlockSpec(memory_space=pl.ANY),
        scratch_shapes=[
            pltpu.SemaphoreType.DMA((peers,)),
            pltpu.SemaphoreType.DMA((peers,)),
            pltpu.SemaphoreType.DMA,
        ],
        compiler_params=pltpu.CompilerParams(collective_id=ident, has_side_effects=True),
        name="exchange",
    )(outgoing)


def operator_pattern(height, depth):
    half = TAPS // 2
    pattern = np.zeros((TAPS * TAPS, 2, height, depth), np.float32)
    for v in range(TAPS):
        for a in range(height):
            for s in range(height):
                if abs(a - s) <= half:
                    pattern[(a - s + half) * TAPS + v, 0, a, v * height + s] = 1.0
                    pattern[(s - a + half) * TAPS + v, 1, a, v * height + s] = 1.0
    return pattern.reshape(TAPS * TAPS, -1)


def build_operators(pool, height, depth):
    kernels = jnp.sum(pool[:, 0, :, :, None] * pool[:, 1, :, None, :], axis=1) / NPSF
    kernels = kernels.reshape(pool.shape[0], TAPS * TAPS)
    full = jnp.dot(kernels, operator_pattern(height, depth), precision=lax.Precision.HIGHEST)
    full = full.reshape(pool.shape[0], 2, height, depth)
    coarse = lax.reduce_precision(full, 8, 7)
    return jnp.concatenate([coarse, full - coarse], axis=2).astype(BF16)


def body(model, exposures, inv_var, step_size, psf_taps, exp_batch, send_plane, send_row, send_cover, use_slot,
         use_start, use_stop, foot_lo, foot_hi):
    tile_count, band_count, tile_rows, columns = model.shape
    count, height, _ = exposures.shape
    peers, capacity = send_plane.shape
    rows_each = capacity * height // 2
    total = tile_count * band_count * tile_rows
    packed_rows = peers * rows_each
    own_banks, width = psf_taps.shape
    extra = -(-own_banks // 16) * 16
    slots = peers * capacity
    depth = -(-TAPS * height // 128) * 128
    unroll = 8 if count % 8 == 0 else 1

    shaped = psf_taps.reshape(own_banks, 2 * NPSF, TAPS)
    shaped = shaped / jnp.sum(shaped, axis=-1, keepdims=True)
    banks = shaped.reshape(own_banks, width).astype(BF16)
    banks = jnp.pad(banks, ((0, extra - own_banks), (0, columns - width)))

    image_scratch = pltpu.VMEM((total + height, columns), F32)
    packed_scratch = pltpu.VMEM((packed_rows + height, columns), F32)

    current = model.reshape(total, columns)
    outbound, begin, source = pl.pallas_call(
        functools.partial(first_kernel, rows_each, tile_rows, height),
        out_shape=(
            jax.ShapeDtypeStruct((peers, rows_each + extra, columns), BF16),
            jax.ShapeDtypeStruct((slots,), jnp.int32),
            jax.ShapeDtypeStruct((slots,), jnp.int32),
        ),
        in_specs=[smem()] * 6 + [vmem()] * 2,
        out_specs=(vmem(), smem(), smem()),
        scratch_shapes=[image_scratch, packed_scratch, pltpu.SMEM((slots + 1,), jnp.int32)],
        name="first_pack",
    )(send_plane, send_row, send_cover, use_slot, use_start, use_stop, current, banks)
    residual = None
    operators = None
    for sweep in range(ITERS):
        arrived = exchange(outbound, 0 if sweep == 0 else 1)
        if sweep == 0:
            pool = arrived[:, rows_each : rows_each + own_banks, :width].astype(F32)
            operators = build_operators(pool.reshape(peers * own_banks, 2, NPSF, TAPS), height, depth)
        residual, outgoing = pl.pallas_call(
            functools.partial(exposure_kernel, rows_each, unroll),
            out_shape=(
                jax.ShapeDtypeStruct(exposures.shape, F32),
                jax.ShapeDtypeStruct((peers, rows_each, columns), BF16),
            ),
            in_specs=[smem()] * 6 + [vmem()] * 3,
            out_specs=(vmem(), vmem()),
            scratch_shapes=[
                pltpu.VMEM((packed_rows + 2 * height, columns), F32),
                pltpu.VMEM(((count + 1) * height, columns), F32),
                pltpu.VMEM((unroll, depth, columns), BF16),
                pltpu.VMEM((unroll, depth, columns), BF16),
            ],
            name="exposures",
        )(use_slot, use_start, exp_batch, inv_var, begin, source, arrived, operators, exposures)
        returned = exchange(outgoing, 1)
        last = sweep == ITERS - 1
        updated_shape = jax.ShapeDtypeStruct((total, columns), F32)
        outbound_shape = jax.ShapeDtypeStruct((peers, rows_each, columns), BF16)
        result = pl.pallas_call(
            functools.partial(tile_kernel, rows_each, tile_rows, height, band_count, last),
            out_shape=updated_shape if last else (updated_shape, outbound_shape),
            in_specs=[smem()] * 6 + [vmem()] * 2,
            out_specs=vmem() if last else (vmem(), vmem()),
            scratch_shapes=[image_scratch, packed_scratch] + ([] if last else [image_scratch, packed_scratch]),
            name="tiles_last" if last else "tiles",
        )(send_plane, send_row, send_cover, foot_lo, foot_hi, step_size, current, returned)
        if last:
            current = result
        else:
            current, outbound = result
    return current.reshape(model.shape), residual


def solution(mesh):
    both = ("groups", "sky")
    return jax.shard_map(
        body,
        mesh=mesh,
        in_specs=(
            P(both, None, None, None),
            P(both, None, None),
            P(both),
            P(),
            P(both, None),
            P(both),
            P(both, None),
            P(both, None),
            P(both, None),
            P(both, None),
            P(both, None),
            P(both, None),
            P(both),
            P(both),
        ),
        out_specs=(P(both, None, None, None), P(both, None, None)),
        check_vma=False,
    )
```

```python
import functools

import jax
import jax.numpy as jnp
import numpy as np
from jax import lax
from jax.experimental import pallas as pl
from jax.experimental.pallas import tpu as pltpu
from jax.sharding import PartitionSpec as P

NPSF = 4
TAPS = 7
ITERS = 2
F32 = jnp.float32
BF16 = jnp.bfloat16


def vmem():
    return pl.BlockSpec(memory_space=pltpu.VMEM)


def smem():
    return pl.BlockSpec(memory_space=pltpu.SMEM)


def pack_rows(image, packed, plane, row, cover, rows_each, tile_rows, height):
    peers, capacity = plane.shape

    def one_peer(o, carry):
        offset = o * rows_each
        for c in range(capacity):
            source = jnp.maximum(plane[o, c], 0) * tile_rows + row[o, c]
            packed[pl.ds(offset, height), :] = image[pl.ds(source, height), :]
            offset = offset + cover[o, c]
        return carry

    lax.fori_loop(0, peers, one_peer, 0)


def emit_packed(packed, out, rows_each):
    def one_peer(o, carry):
        start = pl.multiple_of(o * rows_each, 16)
        out[o, pl.ds(0, rows_each), :] = packed[pl.ds(start, rows_each), :].astype(BF16)
        return carry

    lax.fori_loop(0, out.shape[0], one_peer, 0)


def first_kernel(rows_each, tile_rows, height, plane, row, cover, model, banks, out, image, packed):
    total = model.shape[0]
    image[pl.ds(0, total), :] = model[...]
    image[pl.ds(total, height), :] = jnp.zeros((height, model.shape[1]), F32)
    pack_rows(image, packed, plane, row, cover, rows_each, tile_rows, height)
    emit_packed(packed, out, rows_each)
    extra = banks.shape[0]

    def add_banks(o, carry):
        out[o, pl.ds(rows_each, extra), :] = banks[...]
        return carry

    lax.fori_loop(0, out.shape[0], add_banks, 0)


def tile_kernel(rows_each, tile_rows, height, band_count, last, plane, row, cover, lo, hi, step, current,
                returned, *rest):
    if last:
        updated, grad, arrived = rest
    else:
        updated, out, grad, arrived, image, packed = rest
    total, columns = current.shape
    peers, capacity = plane.shape

    def clear(i, carry):
        start = pl.multiple_of(i * 64, 64)
        grad[pl.ds(start, 64), :] = jnp.zeros((64, columns), F32)
        return carry

    lax.fori_loop(0, total // 64, clear, 0)
    grad[pl.ds(total, height), :] = jnp.zeros((height, columns), F32)

    def widen(o, carry):
        start = pl.multiple_of(o * rows_each, 16)
        arrived[pl.ds(start, rows_each), :] = returned[o].astype(F32)
        return carry

    lax.fori_loop(0, peers, widen, 0)
    arrived[pl.ds(peers * rows_each, height), :] = jnp.zeros((height, columns), F32)
    position = lax.broadcasted_iota(jnp.int32, (height, columns), 0)

    def one_peer(o, carry):
        offset = o * rows_each
        for c in range(capacity):
            target = jnp.maximum(plane[o, c], 0) * tile_rows + row[o, c]
            count = cover[o, c]
            part = jnp.where(position < count, arrived[pl.ds(offset, height), :], 0.0)
            grad[pl.ds(target, height), :] += part
            offset = offset + count
        return carry

    lax.fori_loop(0, peers, one_peer, 0)
    tile_position = lax.broadcasted_iota(jnp.int32, (tile_rows, columns), 0)

    def one_plane(p, carry):
        tile = p // band_count
        start = pl.multiple_of(p * tile_rows, 8)
        here = pl.ds(start, tile_rows)
        moved = jnp.maximum(current[here, :] - step[p % band_count] * grad[here, :], 0.0)
        moved = jnp.where((tile_position >= lo[tile]) & (tile_position < hi[tile]), moved, 0.0)
        updated[here, :] = moved
        if not last:
            image[here, :] = moved
        return carry

    lax.fori_loop(0, total // tile_rows, one_plane, 0)
    if not last:
        image[pl.ds(total, height), :] = jnp.zeros((height, columns), F32)
        pack_rows(image, packed, plane, row, cover, rows_each, tile_rows, height)
        emit_packed(packed, out, rows_each)


def spread(value, target, direction, masks):
    height, columns = value.shape
    half = TAPS // 2
    for v in range(TAPS):
        shift = direction * (v - half)
        part = value
        if shift != 0:
            part = jnp.where(masks[shift + half], pltpu.roll(value, shift % columns, 1), 0.0)
        target[pl.ds(v * height, height), :] = part.astype(BF16)


def apply(operators, bank, way, shifted):
    operator = jnp.concatenate([operators[bank, 0, way], operators[bank, 1, way]], axis=0)
    both = jnp.dot(operator, shifted, preferred_element_type=F32)
    height = both.shape[0] // 2
    return both[:height] + both[height:]


def exposure_kernel(rows_each, unroll, last, at, first, batch, weight, begin, source, arrived, operators, observed,
                    *rest):
    if last:
        residual, out, gathered, stamps, forward, backward = rest
    else:
        out, gathered, stamps, forward, backward = rest
    count, height, columns = observed.shape
    peers = out.shape[0]
    meets = at.shape[0]
    capacity = begin.shape[0] // peers
    half = TAPS // 2

    gathered[pl.ds(0, height), :] = jnp.zeros((height, columns), F32)
    gathered[pl.ds(height + peers * rows_each, height), :] = jnp.zeros((height, columns), F32)
    stamps[pl.ds(count * height, height), :] = jnp.zeros((height, columns), F32)
    used = TAPS * height
    spare = forward.shape[1] - used
    if spare:
        for i in range(unroll):
            forward[i, pl.ds(used, spare), :] = jnp.zeros((spare, columns), BF16)
            backward[i, pl.ds(used, spare), :] = jnp.zeros((spare, columns), BF16)

    def widen(o, carry):
        here = pl.multiple_of(o * rows_each + height, 8)
        gathered[pl.ds(here, rows_each), :] = arrived[o, pl.ds(0, rows_each), :].astype(F32)
        return carry

    lax.fori_loop(0, peers, widen, 0)
    position = lax.broadcasted_iota(jnp.int32, (height, columns), 0)
    lane = lax.broadcasted_iota(jnp.int32, (height, columns), 1)
    masks = [
        (lane >= shift) if shift > 0 else (lane < columns + shift) for shift in range(-half, half + 1)
    ]

    def assemble(e):
        value = None
        for k in range(meets):
            piece = gathered[pl.ds(at[k, e], height), :]
            value = piece if value is None else jnp.where(position >= first[k, e], piece, value)
        return value

    def group(g, carry):
        which = [g * unroll + i for i in range(unroll)]
        for i, e in enumerate(which):
            spread(assemble(e), forward.at[i], 1, masks)
        for i, e in enumerate(which):
            predicted = apply(operators, batch[e], 0, forward[i])
            error = weight[e] * (predicted - observed[e].astype(F32))
            if last:
                residual[e] = error
            spread(error, backward.at[i], -1, masks)
        for i, e in enumerate(which):
            here = pl.multiple_of(e * height, 8)
            stamps[pl.ds(here, height), :] = apply(operators, batch[e], 1, backward[i])
        return carry

    lax.fori_loop(0, count // unroll, group, 0)

    def give(o, carry):
        for c in range(capacity):
            name = o * capacity + c
            gathered[pl.ds(begin[name], height), :] = stamps[pl.ds(source[name], height), :]
        return carry

    lax.fori_loop(0, peers, give, 0)
    emit_packed(gathered, out, rows_each)


def slot_tables(rows_each, height, peers, capacity, use_slot, use_start, use_stop):
    slots = peers * capacity
    names, start, stop = use_slot.T, use_start.T, use_stop.T
    alive = names >= 0
    first = jnp.where(alive, start, height)
    flat = names.reshape(-1)
    length = jnp.where(alive, stop - start, 0).reshape(-1)
    every = jnp.concatenate([jnp.arange(slots, dtype=jnp.int32), flat])
    peer = jnp.maximum(every, 0) // capacity
    earlier = (flat[None, :] >= (peer * capacity)[:, None]) & (flat[None, :] < every[:, None])
    begin = peer * rows_each + jnp.sum(jnp.where(earlier, length[None, :], 0), axis=1)
    row = (jnp.arange(names.shape[1], dtype=jnp.int32) * height)[None, :] + start
    same = flat[None, :] == jnp.arange(slots, dtype=jnp.int32)[:, None]
    source = jnp.sum(jnp.where(same, row.reshape(1, -1), 0), axis=1)
    at = height + jnp.where(alive, begin[slots:].reshape(names.shape) - first, 0)
    return at, first, begin[:slots], source


def partner(me, i, peers):
    if peers & (peers - 1):
        return lax.rem(me + i, peers)
    other = me
    bit = 1
    while bit < peers:
        if i & bit:
            other = other + (1 - 2 * lax.rem(me // bit, 2)) * bit
        bit *= 2
    return other


def exchange_kernel(outgoing, incoming, send_sems, recv_sems, own_sem):
    me = lax.axis_index("sky")
    peers = outgoing.shape[0]
    order = [base + d for base in range(0, peers, 4) for d in (2, 0, 3, 1) if 0 < base + d < peers]
    barrier = pltpu.get_barrier_semaphore()
    for i in order:
        pl.semaphore_signal(
            barrier, inc=1, device_id={"sky": partner(me, i, peers)}, device_id_type=pl.DeviceIdType.MESH
        )
    pl.semaphore_wait(barrier, peers - 1)
    copies = []
    for i in order:
        to = partner(me, i, peers)
        copy = pltpu.make_async_remote_copy(
            src_ref=outgoing.at[to],
            dst_ref=incoming.at[me],
            send_sem=send_sems.at[i],
            recv_sem=recv_sems.at[i],
            device_id={"sky": to},
            device_id_type=pl.DeviceIdType.MESH,
        )
        copy.start()
        copies.append(copy)
    own = pltpu.make_async_copy(outgoing.at[me], incoming.at[me], own_sem)
    own.start()
    own.wait()
    for copy in copies:
        copy.wait()


def exchange(outgoing, ident):
    peers = outgoing.shape[0]
    return pl.pallas_call(
        exchange_kernel,
        out_shape=jax.ShapeDtypeStruct(outgoing.shape, outgoing.dtype),
        in_specs=[pl.BlockSpec(memory_space=pl.ANY)],
        out_specs=pl.BlockSpec(memory_space=pl.ANY),
        scratch_shapes=[
            pltpu.SemaphoreType.DMA((peers,)),
            pltpu.SemaphoreType.DMA((peers,)),
            pltpu.SemaphoreType.DMA,
        ],
        compiler_params=pltpu.CompilerParams(collective_id=ident, has_side_effects=True),
        name="exchange",
    )(outgoing)


def operator_pattern(height, depth):
    half = TAPS // 2
    pattern = np.zeros((TAPS * TAPS, 2, height, depth), np.float32)
    for v in range(TAPS):
        for a in range(height):
            for s in range(height):
                if abs(a - s) <= half:
                    pattern[(a - s + half) * TAPS + v, 0, a, v * height + s] = 1.0
                    pattern[(s - a + half) * TAPS + v, 1, a, v * height + s] = 1.0
    return pattern.reshape(TAPS * TAPS, -1)


def point_spread(psf_taps):
    own_banks = psf_taps.shape[0]
    taps = psf_taps.reshape(own_banks, 2, NPSF, TAPS)
    taps = lax.reduce_precision(taps / jnp.sum(taps, axis=-1, keepdims=True), 8, 7)
    kernels = jnp.sum(taps[:, 0, :, :, None] * taps[:, 1, :, None, :], axis=1) / NPSF
    kernels = kernels.reshape(own_banks, TAPS * TAPS)
    coarse = lax.reduce_precision(kernels, 8, 7)
    return jnp.concatenate([coarse, kernels - coarse], axis=1).astype(BF16)


def build_operators(halves, height, depth):
    pattern = jnp.asarray(operator_pattern(height, depth), BF16)
    full = jnp.dot(halves.reshape(-1, TAPS * TAPS), pattern, preferred_element_type=F32).astype(BF16)
    return full.reshape(-1, 2, 2, height, depth)


def body(model, exposures, inv_var, step_size, psf_taps, exp_batch, send_plane, send_row, send_cover, use_slot,
         use_start, use_stop, foot_lo, foot_hi):
    tile_count, band_count, tile_rows, columns = model.shape
    count, height, _ = exposures.shape
    peers, capacity = send_plane.shape
    rows_each = capacity * height // 2
    total = tile_count * band_count * tile_rows
    packed_rows = peers * rows_each
    own_banks = psf_taps.shape[0]
    extra = -(-own_banks // 16) * 16
    depth = -(-TAPS * height // 128) * 128
    unroll = 16 if count % 16 == 0 else 1

    banks = point_spread(psf_taps)
    width = banks.shape[1]
    banks = jnp.pad(banks, ((0, extra - own_banks), (0, columns - width)))
    at, first, begin, source = slot_tables(rows_each, height, peers, capacity, use_slot, use_start, use_stop)

    image_scratch = pltpu.VMEM((total + height, columns), F32)
    packed_scratch = pltpu.VMEM((packed_rows + height, columns), F32)

    current = model.reshape(total, columns)
    outbound = pl.pallas_call(
        functools.partial(first_kernel, rows_each, tile_rows, height),
        out_shape=jax.ShapeDtypeStruct((peers, rows_each + extra, columns), BF16),
        in_specs=[smem()] * 3 + [vmem()] * 2,
        out_specs=vmem(),
        scratch_shapes=[image_scratch, packed_scratch],
        name="first_pack",
    )(send_plane, send_row, send_cover, current, banks)
    residual = None
    operators = None
    for sweep in range(ITERS):
        arrived = exchange(outbound, 0 if sweep == 0 else 1)
        if sweep == 0:
            halves = arrived[:, rows_each : rows_each + own_banks, :width]
            operators = build_operators(halves, height, depth)
        last = sweep == ITERS - 1
        residual_shape = jax.ShapeDtypeStruct(exposures.shape, F32)
        outgoing_shape = jax.ShapeDtypeStruct((peers, rows_each, columns), BF16)
        result = pl.pallas_call(
            functools.partial(exposure_kernel, rows_each, unroll, last),
            out_shape=(residual_shape, outgoing_shape) if last else outgoing_shape,
            in_specs=[smem()] * 6 + [vmem()] * 3,
            out_specs=(vmem(), vmem()) if last else vmem(),
            scratch_shapes=[
                pltpu.VMEM((packed_rows + 2 * height, columns), F32),
                pltpu.VMEM(((count + 1) * height, columns), F32),
                pltpu.VMEM((unroll, depth, columns), BF16),
                pltpu.VMEM((unroll, depth, columns), BF16),
            ],
            name="exposures_last" if last else "exposures",
        )(at, first, exp_batch, inv_var, begin, source, arrived, operators, exposures)
        if last:
            residual, outgoing = result
        else:
            outgoing = result
        returned = exchange(outgoing, 1)
        updated_shape = jax.ShapeDtypeStruct((total, columns), F32)
        outbound_shape = jax.ShapeDtypeStruct((peers, rows_each, columns), BF16)
        result = pl.pallas_call(
            functools.partial(tile_kernel, rows_each, tile_rows, height, band_count, last),
            out_shape=updated_shape if last else (updated_shape, outbound_shape),
            in_specs=[smem()] * 6 + [vmem()] * 2,
            out_specs=vmem() if last else (vmem(), vmem()),
            scratch_shapes=[image_scratch, packed_scratch] + ([] if last else [image_scratch, packed_scratch]),
            name="tiles_last" if last else "tiles",
        )(send_plane, send_row, send_cover, foot_lo, foot_hi, step_size, current, returned)
        if last:
            current = result
        else:
            current, outbound = result
    return current.reshape(model.shape), residual


def solution(mesh):
    both = ("groups", "sky")
    return jax.shard_map(
        body,
        mesh=mesh,
        in_specs=(
            P(both, None, None, None),
            P(both, None, None),
            P(both),
            P(),
            P(both, None),
            P(both),
            P(both, None),
            P(both, None),
            P(both, None),
            P(both, None),
            P(both, None),
            P(both, None),
            P(both),
            P(both),
        ),
        out_specs=(P(both, None, None, None), P(both, None, None)),
        check_vma=False,
    )
```
